32 devices in a mesh: fsdp: 2 (over y), ctx: 16 (over z, x, core).
Axes of the slice: x: 2, y: 2, z: 4, core: 2. Of those that a mesh axis runs over, the one named last changes fastest.
Arguments:
- block_input: bfloat16 [2, 2048, 1024], P('fsdp', 'ctx'), may hold values from -6 to 6
- doc_lengths: int32 [2, 8], P('fsdp'), may hold values from 1 to 512, 2048 in all within a row
- mixer_weight: bfloat16 [1024, 4096], P('fsdp'), may hold values from -0.1875 to 0.1875
- decay_weight: bfloat16 [1024, 16], P('fsdp'), may hold values from -0.1875 to 0.1875
- head_gate_weight: bfloat16 [1024, 2048], P('fsdp'), may hold values from -0.1875 to 0.1875
- merge_weight: bfloat16 [2048, 1024], P('fsdp'), may hold values from -0.125 to 0.125
- feed_gate: bfloat16 [1024, 2816], P('fsdp'), may hold values from -0.1875 to 0.1875
- feed_up: bfloat16 [1024, 2816], P('fsdp'), may hold values from -0.1875 to 0.1875
- feed_down: bfloat16 [2816, 1024], P('fsdp'), may hold values from -0.109375 to 0.109375
- conv_weight: bfloat16 [4, 4096], P(None, 'fsdp'), may hold values from -2 to 2
- first_gain: bfloat16 [1024], P('fsdp'), may hold values from 0.5 to 1.5
- head_gain: bfloat16 [256], P('fsdp'), may hold values from 0.5 to 1.5
- second_gain: bfloat16 [1024], P('fsdp'), may hold values from 0.5 to 1.5
- log_rate: bfloat16 [8], P('fsdp'), may hold values from 0 to 1.5
- step_bias: bfloat16 [8], P('fsdp'), may hold values from -9 to -2
- output_cotangent: bfloat16 [2, 2048, 1024], P('fsdp', 'ctx'), may hold values from -6 to 6
Outputs:
- block_output: float32 [2, 2048, 1024], P('fsdp', 'ctx')
- input_grad: float32 [2, 2048, 1024], P('fsdp', 'ctx')
- mixer_grad: float32 [1024, 4096], P('fsdp')
- decay_grad: float32 [1024, 16], P('fsdp')
- head_gate_grad: float32 [1024, 2048], P('fsdp')
- merge_grad: float32 [2048, 1024], P('fsdp')
- feed_gate_grad: float32 [1024, 2816], P('fsdp')
- feed_up_grad: float32 [1024, 2816], P('fsdp')
- feed_down_grad: float32 [2816, 1024], P('fsdp')
- conv_grad: float32 [4, 4096], P(None, 'fsdp')
- first_gain_grad: float32 [1024], P('fsdp')
- head_gain_grad: float32 [256], P('fsdp')
- second_gain_grad: float32 [1024], P('fsdp')
- log_rate_grad: float32 [8], P('fsdp')
- step_bias_grad: float32 [8], P('fsdp')
The draws below stay inside these ranges and needn't reach their ends.
Inputs may be any that keep to these rules, and one draw needn't show every extreme that they name: `doc_lengths`: row s holds the lengths of the 8 documents packed in order into stream s; each row sums to 2048, and its longest document has exactly 512 tokens.
All inputs are finite; a program needn't handle non-finite values.
Results may differ from the reference program's by a relative error of at most 0.035.
Values may be sent and summed in bfloat16 or wider, within the bound.
No kernel may reach another device: no remote copies, remote signals or barrier semaphores. Data moves between devices by JAX's collectives and lax.ppermute only.
A program may use at most 320 MiB of HBM per device.

```python
import math
from functools import partial
import jax
import jax.numpy as jnp
import numpy as np
from jax import lax

D = 1024
H = 8
DK = 128
DV = 256
FF = 2816
KCONV = 4
BLOCK = 64
VPART = 64
DOCS = 8
STREAM = 2048
MOST = 512
N_FSDP = 2


def levels(own_key, extent, cuts, low, top_value):
    loudness = 1.0
    for axis_at, shards_of in cuts:
        heights = jax.random.uniform(jax.random.fold_in(jax.random.fold_in(own_key, 6), axis_at), (shards_of,), jnp.float32, low / len(cuts), top_value / len(cuts))
        loudness = loudness * jnp.repeat(jnp.exp(heights), extent[axis_at] // shards_of).reshape((-1,) + (1,) * (len(extent) - 1 - axis_at))
    return loudness


def length_profile(count, total, bound, skew):
    loads = [(1 << 20) // math.isqrt(grade ** skew) + 1 for grade in range(2, count + 1)]
    rest, given = total - bound - (count - 1), [1] * (count - 1)
    while rest > 0:
        movable = [i for i in range(count - 1) if given[i] < bound]
        mass, budget = sum([loads[i] for i in movable]), rest
        for i in movable:
            addition = min(bound - given[i], max(1, budget * loads[i] // mass), rest)
            given[i] = given[i] + addition
            rest = rest - addition
    return np.array([bound] + given)


def uneven(stream_key, number_of, total, bound, lean):
    if number_of == 2:
        one = jax.random.randint(stream_key, (), max(1, total - bound), min(bound, total - 1) + 1)
        return jnp.stack([one, total - one])
    lengths = jnp.asarray(length_profile(number_of, total, bound, lean), jnp.int32)
    couples = (number_of - 1) // 2
    source_of, sink = lengths[1:1 + 2 * couples:2], lengths[2:2 + 2 * couples:2]
    room = jnp.minimum(source_of - 1, bound - sink)
    moved = jax.random.randint(jax.random.fold_in(stream_key, 1), (couples,), 0, 1 << 20) % (room + 1)
    lengths = lengths.at[1:1 + 2 * couples:2].set(source_of - moved).at[2:2 + 2 * couples:2].set(sink + moved)
    return lengths[jax.random.permutation(jax.random.fold_in(stream_key, 2), number_of)]


def bell_draw(rng, dims, deviation, bound, split=(), held_as=jnp.bfloat16):
    values = deviation * jax.random.normal(rng, dims, jnp.float32)
    if split:
        values = values * levels(rng, dims, split, -0.22, 0.18)
    return jnp.clip(values, -bound, bound).astype(held_as)


def setup_inputs(seed: int = 0) -> dict:
    streams_of = jax.random.split(jax.random.key(seed), 17)
    return {
        "block_input": bell_draw(streams_of[0], (N_FSDP, STREAM, D), 1.0, 6.0, ((0, 2), (1, 16))),
        "doc_lengths": jax.vmap(lambda own: uneven(own, DOCS, STREAM, MOST, 2))(jax.random.split(streams_of[1], N_FSDP)).reshape((N_FSDP, DOCS)).astype(jnp.int32),
        "mixer_weight": bell_draw(streams_of[2], (D, 2 * H * DK + H * DV), D ** -0.5, 0.1875, ((0, 2),)),
        "decay_weight": bell_draw(streams_of[3], (D, 2 * H), D ** -0.5, 0.1875, ((0, 2),)),
        "head_gate_weight": bell_draw(streams_of[4], (D, H * DV), D ** -0.5, 0.1875, ((0, 2),)),
        "merge_weight": bell_draw(streams_of[5], (H * DV, D), (H * DV) ** -0.5, 0.125, ((0, 2),)),
        "feed_gate": bell_draw(streams_of[6], (D, FF), D ** -0.5, 0.1875, ((0, 2),)),
        "feed_up": bell_draw(streams_of[7], (D, FF), D ** -0.5, 0.1875, ((0, 2),)),
        "feed_down": bell_draw(streams_of[8], (FF, D), FF ** -0.5, 0.109375, ((0, 2),)),
        "conv_weight": bell_draw(streams_of[9], (KCONV, 2 * H * DK + H * DV), 0.5, 2.0, ((1, 2),)),
        "first_gain": jnp.clip(1.0 + 0.1 * jax.random.normal(streams_of[10], (D,), jnp.float32), 0.5, 1.5).astype(jnp.bfloat16),
        "head_gain": jnp.clip(1.0 + 0.1 * jax.random.normal(streams_of[11], (DV,), jnp.float32), 0.5, 1.5).astype(jnp.bfloat16),
        "second_gain": jnp.clip(1.0 + 0.1 * jax.random.normal(streams_of[12], (D,), jnp.float32), 0.5, 1.5).astype(jnp.bfloat16),
        "log_rate": jnp.clip(1.5 * jax.random.uniform(streams_of[13], (H,), jnp.float32) ** levels(streams_of[13], (H,), ((0, 2),), -0.2, 0.2), 0.0, 1.5).astype(jnp.bfloat16),
        "step_bias": jnp.clip(-9.0 + 7.0 * jax.random.uniform(streams_of[14], (H,), jnp.float32) ** levels(streams_of[14], (H,), ((0, 2),), -0.2, 0.2), -9.0, -2.0).astype(jnp.bfloat16),
        "output_cotangent": bell_draw(streams_of[15], (N_FSDP, STREAM, D), 1.0, 6.0, ((0, 2), (1, 16))),
    }


EPS_NORM = 1e-05
EPS_UNIT = 1e-06
HIGHEST_PRECISION = lax.Precision.HIGHEST

@jax.custom_vjp
def low(v):
    return lax.optimization_barrier(v.astype(jnp.bfloat16)).astype(jnp.float32)

@jax.custom_vjp
def low_back(v):
    return v

def low_keep(v):
    return (low(v), None)

def low_pass(kept, grad):
    return (grad,)

def back_keep(v):
    return (v, None)

def back_low(kept, grad):
    return (low(grad),)
low.defvjp(low_keep, low_pass)
low_back.defvjp(back_keep, back_low)

def matmul(left, right):
    return jnp.dot(left.astype(jnp.float32), right.astype(jnp.float32), precision=HIGHEST_PRECISION, preferred_element_type=jnp.float32)

def rms_scale(entries, scaling):
    factor = lax.rsqrt(lax.optimization_barrier(jnp.mean(entries * entries, axis=-1, keepdims=True)) + EPS_NORM)
    return entries * factor * scaling

def unit_rows(entries):
    return entries * lax.rsqrt(lax.optimization_barrier(jnp.sum(entries * entries, axis=-1, keepdims=True)) + EPS_UNIT)

def doc_numbers(positions, bounds):
    counted = lax.optimization_barrier(jnp.sum((positions[:, None] >= bounds[None, :]).astype(jnp.int32), axis=1)).astype(jnp.int32)
    return jnp.where(positions >= 0, counted, -1).astype(jnp.int32)

def mix_inputs(extended, gates_in, conv_full, rate_full, bias_full, tap_valid):
    token_count = gates_in.shape[0]
    summed_taps = jnp.zeros((token_count, extended.shape[1]), jnp.float32)
    for offset in range(KCONV):
        begin = KCONV - 1 - offset
        summed_taps = summed_taps + conv_full[offset] * extended[begin:begin + token_count] * tap_valid[offset][:, None]
    activated = jax.nn.silu(summed_taps)
    query = unit_rows(activated[:, :H * DK].reshape(token_count, H, DK))
    key_rows = unit_rows(activated[:, H * DK:2 * H * DK].reshape(token_count, H, DK))
    values = activated[:, 2 * H * DK:]
    beta_gate = jax.nn.sigmoid(gates_in[:, :H])
    log_decay = -jnp.exp(rate_full) * jax.nn.softplus(gates_in[:, H:] + bias_full)
    return (query, key_rows, values, beta_gate, log_decay)

def pack_pairs(query, key_rows, values, beta_gate, log_decay):
    groups = DV // VPART
    token_count = query.shape[0]
    head_query = jnp.repeat(query, groups, axis=1)
    head_key = jnp.repeat(key_rows, groups, axis=1)
    value_parts = values.reshape(token_count, H * groups, VPART)
    beta_parts = jnp.repeat(beta_gate, groups, axis=1)[:, :, None]
    decay_parts = jnp.repeat(log_decay, groups, axis=1)[:, :, None]
    joined = jnp.concatenate([head_query, head_key, value_parts, beta_parts, decay_parts], axis=2)
    return jnp.transpose(joined, (1, 2, 0))

def mixer_item(packed_item, document_ids):
    length = packed_item.shape[1]
    token_rows = packed_item.T
    query = token_rows[:, :DK]
    key_rows = token_rows[:, DK:2 * DK]
    values = token_rows[:, 2 * DK:2 * DK + VPART]
    beta_gate = token_rows[:, 2 * DK + VPART]
    log_decay = token_rows[:, 2 * DK + VPART + 1]
    block_count = length // BLOCK
    before = jnp.concatenate([jnp.full((1,), -1, jnp.int32), document_ids[BLOCK - 1::BLOCK][:-1]])
    blocks = (query.reshape(block_count, BLOCK, DK), key_rows.reshape(block_count, BLOCK, DK), values.reshape(block_count, BLOCK, VPART), beta_gate.reshape(block_count, BLOCK), log_decay.reshape(block_count, BLOCK), document_ids.reshape(block_count, BLOCK), before)
    positions = jnp.arange(BLOCK)
    lower_mask = positions[:, None] >= positions[None, :]
    strict_mask = (positions[:, None] > positions[None, :]).astype(jnp.float32)
    identity = jnp.eye(BLOCK, dtype=jnp.float32)

    def advance(memory, block_parts):
        query_block, key_block, value_block, beta_block, decay_block, doc_block, doc_before = block_parts
        cumulative = jnp.cumsum(decay_block)
        live_mask = (doc_block[:, None] == doc_block[None, :]) & lower_mask
        decay_ratio = jnp.exp(jnp.where(live_mask, cumulative[:, None] - cumulative[None, :], 0.0)) * live_mask.astype(jnp.float32)
        from_state = jnp.exp(cumulative) * (doc_block == doc_before).astype(jnp.float32)
        to_state = jnp.exp(cumulative[-1] - cumulative) * (doc_block == doc_block[-1]).astype(jnp.float32)
        key_gram = jnp.dot(key_block, key_block.T, precision=HIGHEST_PRECISION)
        coupling = beta_block[:, None] * decay_ratio * key_gram * strict_mask
        right_side = beta_block[:, None] * (value_block - from_state[:, None] * jnp.dot(key_block, memory, precision=HIGHEST_PRECISION))
        pseudo = jax.scipy.linalg.solve_triangular(identity + coupling, right_side, lower=True, unit_diagonal=True)
        scores = decay_ratio * jnp.dot(query_block, key_block.T, precision=HIGHEST_PRECISION)
        output = from_state[:, None] * jnp.dot(query_block, memory, precision=HIGHEST_PRECISION) + jnp.dot(scores, pseudo, precision=HIGHEST_PRECISION)
        updated = from_state[-1] * memory + jnp.dot(key_block.T, to_state[:, None] * pseudo, precision=HIGHEST_PRECISION)
        return (updated, output)
    initial = jnp.zeros((DK, VPART), jnp.float32)
    last_memory, outputs = lax.scan(jax.checkpoint(advance), initial, blocks)
    return outputs.reshape(length, VPART).T

def gated_norm(mixed_rows, head_gate, head_full):
    per_head = mixed_rows.reshape(-1, H, DV)
    factor = lax.rsqrt(lax.optimization_barrier(jnp.mean(per_head * per_head, axis=-1, keepdims=True)) + EPS_NORM)
    gate_rows = jax.nn.silu(head_gate.reshape(-1, H, DV))
    return (per_head * factor * head_full * gate_rows).reshape(-1, H * DV)

def swiglu(gate_pre, up_pre):
    return jax.nn.silu(gate_pre) * up_pre

def reference(block_input, doc_lengths, mixer_weight, decay_weight, head_gate_weight, merge_weight, feed_gate, feed_up, feed_down, conv_weight, first_gain, head_gain, second_gain, log_rate, step_bias, output_cotangent):
    weights = tuple((weight_item.astype(jnp.float32) for weight_item in (mixer_weight, decay_weight, head_gate_weight, merge_weight, feed_gate, feed_up, feed_down, conv_weight, first_gain, head_gain, second_gain, log_rate, step_bias)))
    inputs = block_input.astype(jnp.float32)

    def forward(inputs, mixer_full, decay_full, head_gate_full, merge_full, gate_full, up_full, down_full, conv_full, first_full, head_full, second_full, rate_full, bias_full):
        streams_count = inputs.shape[0]
        length = inputs.shape[1]
        flat_rows = inputs.reshape(-1, D)
        normed_low = low(rms_scale(flat_rows, first_full))
        projected = low_back(low(matmul(normed_low, mixer_full)))
        gates_in = low_back(matmul(normed_low, decay_full))
        head_gate = low_back(matmul(normed_low, head_gate_full))
        positions = jnp.arange(length, dtype=jnp.int32)
        pieces = []
        for stream in range(streams_count):
            bounds = jnp.cumsum(doc_lengths[stream]).astype(jnp.int32)
            document_ids = doc_numbers(positions, bounds)
            tap_valid = jnp.stack([(doc_numbers(positions - offset, bounds) == document_ids).astype(jnp.float32) for offset in range(KCONV)])
            stream_rows = projected[stream * length:(stream + 1) * length]
            extended = jnp.concatenate([jnp.zeros((KCONV - 1, stream_rows.shape[1]), jnp.float32), stream_rows], axis=0)
            stream_gates = gates_in[stream * length:(stream + 1) * length]
            packed = low_back(low(pack_pairs(*mix_inputs(extended, stream_gates, conv_full, rate_full, bias_full, tap_valid))))
            mixed_pairs = lax.map(partial(mixer_item, document_ids=document_ids), packed)
            tokens_view = jnp.transpose(mixed_pairs, (2, 0, 1)).reshape(length, H * DV)
            pieces.append(low_back(low(tokens_view)))
        mixed_rows = jnp.concatenate(pieces, axis=0)
        gated_rows = low(gated_norm(mixed_rows, head_gate, head_full))
        residual = flat_rows + low_back(matmul(gated_rows, merge_full))
        second_low = low(rms_scale(residual, second_full))
        gate_pre = low_back(matmul(second_low, gate_full))
        up_pre = low_back(matmul(second_low, up_full))
        hidden = low(swiglu(gate_pre, up_pre))
        result = residual + low_back(matmul(hidden, down_full))
        return result.reshape(streams_count, length, D)
    result, pullback = jax.vjp(forward, inputs, *weights)
    gradients = pullback(output_cotangent.astype(jnp.float32))
    return (result, gradients[0], gradients[1], gradients[2], gradients[3], gradients[4], gradients[5], gradients[6], gradients[7], gradients[8], gradients[9], gradients[10], gradients[11], gradients[12], gradients[13])
```

```python
import functools

import jax
import jax.numpy as jnp
from jax import lax
from jax.experimental import pallas as pl
from jax.experimental.pallas import tpu as pltpu
from jax.sharding import PartitionSpec as P

H = 8
DK = 128
DV = 256
KCONV = 4
CHUNK = 128
EPS_NORM = 1e-05
EPS_UNIT = 1e-06
BF = jnp.bfloat16
F32 = jnp.float32


def rms_scale(entries, scaling):
    factor = lax.rsqrt(jnp.mean(entries * entries, axis=-1, keepdims=True) + EPS_NORM)
    return entries * factor * scaling


def unit_rows(entries):
    return entries * lax.rsqrt(jnp.sum(entries * entries, axis=-1, keepdims=True) + EPS_UNIT)


def swiglu(gate_pre, up_pre):
    return jax.nn.silu(gate_pre) * up_pre


def product(left, right):
    return jnp.dot(left, right, preferred_element_type=F32)


def dot_nn(a, b):
    return lax.dot_general(
        a.astype(BF), b.astype(BF), (((1,), (0,)), ((), ())), preferred_element_type=F32
    )


def dot_nt(a, b):
    return lax.dot_general(
        a.astype(BF), b.astype(BF), (((1,), (1,)), ((), ())), preferred_element_type=F32
    )


def dot_tn(a, b):
    return lax.dot_general(
        a.astype(BF), b.astype(BF), (((0,), (0,)), ((), ())), preferred_element_type=F32
    )


def halves(a):
    high = a.astype(BF)
    return high, (a - high.astype(F32)).astype(BF)


def dot_fine(a, b):
    return dot_nn(a[0], b[0]) + (dot_nn(a[0], b[1]) + dot_nn(a[1], b[0]))


def grid_indices():
    rows = lax.broadcasted_iota(jnp.int32, (CHUNK, CHUNK), 0)
    columns = lax.broadcasted_iota(jnp.int32, (CHUNK, CHUNK), 1)
    return rows, columns


def unit_lower_inverse(coupling, rows, columns):
    apart = rows ^ columns
    inverse = jnp.where(rows == columns, 1.0, 0.0) - jnp.where(apart == 1, coupling, 0.0)
    size = 2
    while size < CHUNK:
        chosen = (apart >= size) & (apart < 2 * size)
        part = halves(jnp.where(chosen, coupling, 0.0))
        split = halves(inverse)
        inverse = inverse - dot_fine(split, halves(dot_fine(part, split)))
        size *= 2
    return inverse


def decay_table(cols, rows_in, rows, columns):
    live = (cols[:, 4:5] == rows_in[1:2, :]) & (rows >= columns)
    return jnp.where(live, jnp.exp(jnp.where(live, cols[:, 3:4] - rows_in[0:1, :], 0.0)), 0.0)


def mixer_forward_kernel(
    count, q_ref, k_ref, v_ref, cols_ref, rows_ref, out_ref, state_ref, inv_ref, w_ref, z_ref, u_ref, memory
):
    @pl.when(pl.program_id(0) == 0)
    def _():
        memory[...] = jnp.zeros_like(memory)

    rows, columns = grid_indices()
    prepared = []
    for b in range(count):
        at = slice(b * CHUNK, (b + 1) * CHUNK)
        q, k, v = q_ref[at, :], k_ref[at, :], v_ref[at, :]
        cols = cols_ref[at, :]
        ratio = decay_table(cols, rows_ref[b * 8 : b * 8 + 8, :], rows, columns)
        beta, gamma, ending = cols[:, 0:1], cols[:, 1:2], cols[:, 2:3]
        coupling = jnp.where(rows > columns, beta * ratio * dot_nt(k, k), 0.0)
        inverse = unit_lower_inverse(coupling, rows, columns)
        scores = ratio * dot_nt(q, k)
        kf = k.astype(F32)
        w = dot_nn(inverse, (beta * gamma) * kf)
        u_free = dot_nn(inverse, beta * v.astype(F32))
        z = gamma * q.astype(F32) - dot_nn(scores, w)
        out_free = dot_nn(scores, u_free)
        key_end = (ending * kf).astype(BF)
        inv_ref[at, :] = inverse.astype(BF)
        w_ref[at, :] = w.astype(BF)
        z_ref[at, :] = z.astype(BF)
        prepared.append((w, u_free, z, out_free, dot_tn(key_end, w), dot_tn(key_end, u_free), gamma))
    state = memory[...]
    for b in range(count):
        at = slice(b * CHUNK, (b + 1) * CHUNK)
        w, u_free, z, out_free, step, gain, gamma = prepared[b]
        state_ref[b * DK : (b + 1) * DK, :] = state
        low = state.astype(BF)
        out_ref[at, :] = (out_free + dot_nn(z, low)).astype(out_ref.dtype)
        u_ref[at, :] = (u_free - dot_nn(w, low)).astype(BF)
        state = gamma[CHUNK - 1 : CHUNK, :] * state - dot_nn(step, low) + gain
    memory[...] = state


def mixer_backward_kernel(
    count,
    q_ref,
    k_ref,
    v_ref,
    cols_ref,
    rows_ref,
    state_ref,
    inv_ref,
    w_ref,
    z_ref,
    u_ref,
    dout_ref,
    dq_ref,
    dk_ref,
    dv_ref,
    dcols_ref,
    drows_ref,
    carry,
):
    @pl.when(pl.program_id(0) == 0)
    def _():
        carry[...] = jnp.zeros_like(carry)

    rows, columns = grid_indices()
    pulls = []
    for b in range(count):
        at = slice(b * CHUNK, (b + 1) * CHUNK)
        key_end = (cols_ref[at, 2:3] * k_ref[at, :].astype(F32)).astype(BF)
        pulls.append((key_end, dot_tn(w_ref[at, :], key_end), dot_tn(z_ref[at, :], dout_ref[at, :])))
    ends = [None] * count
    grad_state = carry[...]
    for b in reversed(range(count)):
        last = b * CHUNK + CHUNK - 1
        ends[b] = grad_state
        key_end, step, gain = pulls[b]
        grad_state = cols_ref[last : last + 1, 1:2] * grad_state - dot_nn(step, grad_state) + gain
    carry[...] = grad_state
    for b in range(count):
        at = slice(b * CHUNK, (b + 1) * CHUNK)
        q, k, v = q_ref[at, :], k_ref[at, :], v_ref[at, :]
        u, dout = u_ref[at, :], dout_ref[at, :]
        cols = cols_ref[at, :]
        ratio = decay_table(cols, rows_ref[b * 8 : b * 8 + 8, :], rows, columns)
        beta, gamma, ending = cols[:, 0:1], cols[:, 1:2], cols[:, 2:3]
        state = state_ref[b * DK : (b + 1) * DK, :]
        low = state.astype(BF)
        grad_end = ends[b]
        grad_low = grad_end.astype(BF)
        kf = k.astype(F32)
        decayed_gram = ratio * dot_nt(k, k)
        scores = ratio * dot_nt(q, k)
        key_end = pulls[b][0]
        grad_u = dot_tn(scores, dout) + dot_nn(key_end, grad_low)
        grad_right = dot_tn(inv_ref[at, :], grad_u)
        grad_coupling = jnp.where(rows > columns, -dot_nt(grad_right, u), 0.0)
        key_state = dot_nn(k, low)
        query_state = dot_nn(q, low)
        dout_f = dout.astype(F32)
        dv_ref[at, :] = (beta * grad_right).astype(dv_ref.dtype)
        grad_gamma = jnp.sum(dout_f * query_state, axis=1, keepdims=True) - beta * jnp.sum(
            grad_right * key_state, axis=1, keepdims=True
        )
        gram_part = grad_coupling * decayed_gram
        grad_beta = jnp.sum(
            grad_right * (v.astype(F32) - gamma * key_state), axis=1, keepdims=True
        ) + jnp.sum(gram_part, axis=1, keepdims=True)
        grad_scores = dot_nt(dout, u)
        grad_qk = (ratio * grad_scores).astype(BF)
        grad_kk = (beta * ratio * grad_coupling).astype(BF)
        grad_key_end = dot_nt(u, grad_low)
        dq_ref[at, :] = (gamma * dot_nt(dout, low) + dot_nn(grad_qk, k)).astype(dq_ref.dtype)
        dk_ref[at, :] = (
            dot_nt((-beta * gamma) * grad_right, low)
            + dot_tn(grad_qk, q)
            + ending * grad_key_end
            + dot_nn(grad_kk, k)
            + dot_tn(grad_kk, k)
        ).astype(dk_ref.dtype)
        end_part = ending * jnp.sum(grad_key_end * kf, axis=1, keepdims=True)
        table_part = grad_scores * scores + beta * gram_part
        final = gamma[CHUNK - 1 : CHUNK, :] * jnp.sum(
            jnp.sum(grad_end * state, axis=1, keepdims=True), axis=0, keepdims=True
        ) + jnp.sum(end_part, axis=0, keepdims=True)
        grad_sum = jnp.sum(table_part, axis=1, keepdims=True) + grad_gamma * gamma - end_part
        grad_sum = grad_sum + jnp.where(rows[:, 0:1] == CHUNK - 1, final, 0.0)
        lane = lax.broadcasted_iota(jnp.int32, (CHUNK, 8), 1)
        dcols_ref[at, :] = jnp.where(lane == 0, grad_beta, jnp.where(lane == 1, grad_sum, 0.0))
        drows_ref[b * 8 : b * 8 + 8, :] = jnp.broadcast_to(
            -jnp.sum(table_part, axis=0, keepdims=True), (8, CHUNK)
        )


def mixer_forward(q, k, v, cols, rows):
    length, width = v.shape
    count = 4
    span = count * CHUNK
    tokens = lambda n: pl.BlockSpec((span, n), lambda i: (i, 0))
    return pl.pallas_call(
        functools.partial(mixer_forward_kernel, count),
        grid=(length // span,),
        in_specs=[
            tokens(DK),
            tokens(DK),
            tokens(width),
            tokens(8),
            pl.BlockSpec((count * 8, CHUNK), lambda i: (i, 0)),
        ],
        out_specs=[
            tokens(width),
            pl.BlockSpec((count * DK, width), lambda i: (i, 0)),
            tokens(CHUNK),
            tokens(DK),
            tokens(DK),
            tokens(width),
        ],
        out_shape=[
            jax.ShapeDtypeStruct((length, width), BF),
            jax.ShapeDtypeStruct((length // CHUNK * DK, width), F32),
            jax.ShapeDtypeStruct((length, CHUNK), BF),
            jax.ShapeDtypeStruct((length, DK), BF),
            jax.ShapeDtypeStruct((length, DK), BF),
            jax.ShapeDtypeStruct((length, width), BF),
        ],
        scratch_shapes=[pltpu.VMEM((DK, width), F32)],
        compiler_params=pltpu.CompilerParams(dimension_semantics=("arbitrary",)),
        name="mixer_forward",
    )(q, k, v, cols, rows)


def mixer_backward(q, k, v, cols, rows, states, inverse, w, z, u, dout):
    length, width = v.shape
    count = 4
    span = count * CHUNK
    steps = length // span
    back = lambda i: (steps - 1 - i, 0)
    tokens = lambda n: pl.BlockSpec((span, n), back)
    small = pl.BlockSpec((count * 8, CHUNK), back)
    return pl.pallas_call(
        functools.partial(mixer_backward_kernel, count),
        grid=(steps,),
        in_specs=[
            tokens(DK),
            tokens(DK),
            tokens(width),
            tokens(8),
            small,
            pl.BlockSpec((count * DK, width), back),
            tokens(CHUNK),
            tokens(DK),
            tokens(DK),
            tokens(width),
            tokens(width),
        ],
        out_specs=[tokens(DK), tokens(DK), tokens(width), tokens(8), small],
        out_shape=[
            jax.ShapeDtypeStruct((length, DK), BF),
            jax.ShapeDtypeStruct((length, DK), BF),
            jax.ShapeDtypeStruct((length, width), BF),
            jax.ShapeDtypeStruct((length, 8), F32),
            jax.ShapeDtypeStruct((length // CHUNK * 8, CHUNK), F32),
        ],
        scratch_shapes=[pltpu.VMEM((DK, width), F32)],
        compiler_params=pltpu.CompilerParams(dimension_semantics=("arbitrary",)),
        name="mixer_backward",
    )(q, k, v, cols, rows, states, inverse, w, z, u, dout)


def fsdp_stack(shard):
    parts = lax.axis_size("fsdp")
    if parts == 2:
        other = lax.ppermute(shard, "fsdp", [(0, 1), (1, 0)])
        first = lax.axis_index("fsdp") == 0
        return jnp.stack([jnp.where(first, shard, other), jnp.where(first, other, shard)])
    return lax.all_gather(shard, "fsdp")


def fsdp_sum(entries):
    parts = lax.axis_size("fsdp")
    if parts == 2:
        return entries + lax.ppermute(entries, "fsdp", [(0, 1), (1, 0)])
    return lax.psum(entries, "fsdp")


def fsdp_sum_rows(entries):
    parts = lax.axis_size("fsdp")
    if parts == 2:
        half = entries.shape[0] // 2
        first = lax.axis_index("fsdp") == 0
        mine = jnp.where(first, entries[:half], entries[half:])
        theirs = jnp.where(first, entries[half:], entries[:half])
        return mine + lax.ppermute(theirs.astype(BF), "fsdp", [(0, 1), (1, 0)]).astype(F32)
    return lax.psum_scatter(entries, "fsdp", scatter_dimension=0, tiled=True)


def group_exchange(entries, group):
    total = entries.astype(F32)
    size = lax.axis_size("ctx")
    for shift in range(1, group):
        pairs = [(i, i // group * group + (i % group + shift) % group) for i in range(size)]
        total = total + lax.ppermute(entries, "ctx", pairs).astype(F32)
    return total


def weight_pieces(shard):
    parts = lax.axis_size("fsdp")
    height = shard.shape[0]
    if parts != 2:
        return [(0, lax.all_gather(shard, "fsdp", axis=0, tiled=True))]
    size = lax.axis_size("ctx")
    half = height // 2
    core = lax.axis_index("ctx") % 2
    own = lax.axis_index("fsdp") * height
    far = height - own
    sent = lax.dynamic_slice_in_dim(shard, core * half, half, 0)
    direct = lax.ppermute(sent, "fsdp", [(0, 1), (1, 0)])
    passed = lax.ppermute(direct, "ctx", [(i, i ^ 1) for i in range(size)])
    return [(own, shard), (far + core * half, direct), (far + (1 - core) * half, passed)]


def times_pieces(entries, pieces):
    total = None
    for start, piece in pieces:
        part = product(lax.dynamic_slice_in_dim(entries, start, piece.shape[0], 1), piece)
        total = part if total is None else total + part
    return total


def times_pieces_back(entries, pieces):
    height = sum(piece.shape[0] for _, piece in pieces)
    filled = jnp.zeros((entries.shape[0], height), F32)
    for start, piece in pieces:
        part = lax.dot_general(
            entries, piece, (((1,), (1,)), ((), ())), preferred_element_type=F32
        )
        filled = lax.dynamic_update_slice(filled, part, (0, start))
    return filled


def gather_tokens(entries):
    return lax.all_gather(entries, "ctx", axis=0, tiled=True)


def per_device(
    block_input,
    doc_lengths,
    mixer_weight,
    decay_weight,
    head_gate_weight,
    merge_weight,
    feed_gate,
    feed_up,
    feed_down,
    conv_weight,
    first_gain,
    head_gain,
    second_gain,
    log_rate,
    step_bias,
    output_cotangent,
):
    parts = lax.axis_size("fsdp")
    size = lax.axis_size("ctx")
    here = block_input.shape[1]
    length = size * here
    width = H * DV // size
    group = size // H
    keep = 2 * DK // group
    rank = lax.axis_index("ctx")
    home = lax.axis_index("fsdp")
    head = rank // group
    place = rank % group
    features = block_input.shape[2]
    shard_rows = mixer_weight.shape[0]

    x_low = gather_tokens(block_input[0])
    dy_low = gather_tokens(output_cotangent[0])

    conv_cols = conv_weight.shape[1]
    lengths = [first_gain.shape[0], second_gain.shape[0], head_gain.shape[0], log_rate.shape[0], step_bias.shape[0]]
    smalls = fsdp_stack(
        jnp.concatenate([first_gain, second_gain, head_gain, log_rate, step_bias, conv_weight.reshape(-1)])
    ).astype(F32)
    offsets = [0]
    for n in lengths:
        offsets.append(offsets[-1] + n)
    first_full, second_full, head_full, rate_full, bias_full = (
        smalls[:, offsets[i] : offsets[i + 1]].reshape(-1) for i in range(5)
    )
    conv_full = (
        smalls[:, offsets[5] :].reshape(parts, KCONV, conv_cols).transpose(1, 0, 2).reshape(KCONV, -1)
    )

    cut = lambda a, start, n: lax.dynamic_slice_in_dim(a, start, n, 1)
    near = jnp.concatenate(
        [
            cut(mixer_weight, head * DK, DK),
            cut(mixer_weight, H * DK + head * DK, DK),
            cut(mixer_weight, 2 * H * DK + rank * width, width),
            cut(head_gate_weight, rank * width, width),
            cut(decay_weight, head, 1),
            cut(decay_weight, H + head, 1),
        ],
        axis=1,
    )
    columns = fsdp_stack(near).reshape(features, -1)
    conv_here = jnp.concatenate(
        [
            cut(conv_full, head * DK, DK),
            cut(conv_full, H * DK + head * DK, DK),
            cut(conv_full, 2 * H * DK + rank * width, width),
        ],
        axis=1,
    )
    rate_here = lax.dynamic_slice_in_dim(rate_full, head, 1, 0)
    bias_here = lax.dynamic_slice_in_dim(bias_full, head, 1, 0)

    merge_pieces = weight_pieces(merge_weight)
    gate_pieces = weight_pieces(feed_gate)
    up_pieces = weight_pieces(feed_up)
    down_pieces = weight_pieces(feed_down)

    bounds = jnp.cumsum(doc_lengths[0])
    positions = jnp.arange(length, dtype=jnp.int32)
    docs = jnp.sum((positions[:, None] >= bounds[None, :]).astype(jnp.int32), axis=1)
    starts = jnp.sum(
        jnp.where(positions[:, None] >= bounds[None, :], doc_lengths[0][None, :], 0), axis=1
    )
    depth = positions - starts

    x_all = x_low.astype(F32)
    scale_all = lax.rsqrt(jnp.mean(x_all * x_all, axis=-1, keepdims=True) + EPS_NORM)
    normed_low = (x_all * scale_all * first_full).astype(BF)
    inner = 2 * DK + width
    projected_all = product(normed_low, columns)
    projected = projected_all[:, :inner].astype(BF)
    head_gate = projected_all[:, inner : inner + width]
    gates_in = projected_all[:, inner + width :]

    def front(rows, gate_rows, conv_rows, rate, bias):
        summed = conv_rows[0] * rows
        for offset in range(1, KCONV):
            moved = jnp.pad(rows, ((offset, 0), (0, 0)))[:length]
            valid = (depth >= offset).astype(F32)[:, None]
            summed = summed + conv_rows[offset] * moved * valid
        activated = jax.nn.silu(summed)
        query = unit_rows(activated[:, :DK])
        key_rows = unit_rows(activated[:, DK : 2 * DK])
        beta = jax.nn.sigmoid(gate_rows[:, 0])
        decay = -jnp.exp(rate) * jax.nn.softplus(gate_rows[:, 1] + bias)
        return query, key_rows, activated[:, 2 * DK :], beta, decay

    (query, key_rows, values, beta, decay), front_back = jax.vjp(
        front, projected.astype(F32), gates_in, conv_here, rate_here, bias_here
    )
    q_low, k_low, v_low = query.astype(BF), key_rows.astype(BF), values.astype(BF)
    beta_low = beta.astype(BF).astype(F32)
    decay_low = decay.astype(BF).astype(F32)
    chunks = length // CHUNK
    sums = jnp.cumsum(decay_low.reshape(chunks, CHUNK), axis=1)
    doc_rows = docs.reshape(chunks, CHUNK)
    before = jnp.concatenate([jnp.full((1,), -1, jnp.int32), doc_rows[:-1, -1]])
    gamma = jnp.exp(sums) * (doc_rows == before[:, None]).astype(F32)
    ending = jnp.exp(sums[:, -1:] - sums) * (doc_rows == doc_rows[:, -1:]).astype(F32)
    doc_f = doc_rows.astype(F32)
    blank = jnp.zeros_like(sums)
    cols = jnp.stack(
        [beta_low.reshape(chunks, CHUNK), gamma, ending, sums, doc_f, blank, blank, blank], axis=-1
    ).reshape(length, 8)
    rows = jnp.stack([sums, doc_f, blank, blank, blank, blank, blank, blank], axis=1).reshape(
        chunks * 8, CHUNK
    )
    mixed_low, states, inverse, w, z, u = mixer_forward(q_low, k_low, v_low, cols, rows)

    mixed = mixed_low.astype(F32)
    squares = group_exchange(jnp.sum(mixed * mixed, axis=1), group)
    factor = lax.rsqrt(squares / DV + EPS_NORM)[:, None]
    gain_here = lax.dynamic_slice_in_dim(head_full, place * width, width, 0)
    opened = jax.nn.silu(head_gate)
    gated_cols = (mixed * factor * gain_here * opened).astype(BF)
    gated_low = (
        lax.all_to_all(
            gated_cols.reshape(size, here, width), "ctx", split_axis=0, concat_axis=0, tiled=True
        )
        .transpose(1, 0, 2)
        .reshape(here, H * DV)
    )

    inputs = block_input[0].astype(F32)
    residual = inputs + times_pieces(gated_low, merge_pieces)
    second, second_back = jax.vjp(rms_scale, residual, second_full)
    second_low = second.astype(BF)
    second_all = gather_tokens(second_low)
    gate_pre = times_pieces(second_low, gate_pieces)
    up_pre = times_pieces(second_low, up_pieces)
    hidden_full, swiglu_back = jax.vjp(swiglu, gate_pre, up_pre)
    hidden = hidden_full.astype(BF)
    block_output = (residual + times_pieces(hidden, down_pieces))[None]
    cotangent = output_cotangent[0]
    grad_hidden = times_pieces_back(cotangent, down_pieces)
    grad_gate_pre, grad_up_pre = swiglu_back(grad_hidden)
    grad_gate_low = grad_gate_pre.astype(BF)
    grad_up_low = grad_up_pre.astype(BF)
    grad_second = times_pieces_back(grad_gate_low, gate_pieces) + times_pieces_back(
        grad_up_low, up_pieces
    )
    grad_residual_part, second_gain_local = second_back(grad_second)
    grad_residual = cotangent.astype(F32) + grad_residual_part
    grad_branch = grad_residual.astype(BF)
    branch_all = gather_tokens(grad_branch)
    grad_gated = times_pieces_back(grad_branch, merge_pieces).astype(BF)
    grad_cols = lax.all_to_all(
        grad_gated.reshape(here, size, width).transpose(1, 0, 2),
        "ctx",
        split_axis=0,
        concat_axis=0,
        tiled=True,
    ).reshape(length, width)

    feed = feed_gate.shape[1]

    def by_rows(entries):
        n = entries.shape[1]
        return entries.reshape(here, parts, size, n // (parts * size)).transpose(2, 0, 1, 3).reshape(
            size, here, n // size
        )

    def by_cols(entries):
        return entries.reshape(here, size, entries.shape[1] // size).transpose(1, 0, 2)

    sent = jnp.concatenate(
        [by_rows(gated_low), by_rows(hidden), by_cols(grad_gate_low), by_cols(grad_up_low)], axis=2
    )
    dealt = lax.all_to_all(sent, "ctx", split_axis=0, concat_axis=0, tiled=True).reshape(length, -1)
    merge_n, feed_n = H * DV // size, feed // size

    def gram(left, right):
        return lax.dot_general(left, right, (((0,), (0,)), ((), ())), preferred_element_type=F32)

    merge_part = fsdp_sum_rows(gram(dealt[:, :merge_n], branch_all)).astype(BF)
    down_part = fsdp_sum_rows(gram(dealt[:, merge_n : merge_n + feed_n], dy_low)).astype(BF)
    pair_part = fsdp_sum_rows(gram(second_all, dealt[:, merge_n + feed_n :])).astype(BF)
    rows_all = lax.all_gather(jnp.concatenate([merge_part, down_part], axis=0), "ctx")
    pairs_all = lax.all_gather(pair_part, "ctx")
    merge_grad = rows_all[:, : merge_n // parts].reshape(-1, features).astype(F32)
    down_grad = rows_all[:, merge_n // parts :].reshape(-1, features).astype(F32)
    gate_grad = pairs_all[:, :, :feed_n].transpose(1, 0, 2).reshape(shard_rows, feed).astype(F32)
    up_grad = pairs_all[:, :, feed_n:].transpose(1, 0, 2).reshape(shard_rows, feed).astype(F32)

    grad_g = grad_cols.astype(F32)
    along = group_exchange(jnp.sum(mixed * gain_here * opened * grad_g, axis=1), group)[:, None]
    sigma = jax.nn.sigmoid(head_gate)
    common = grad_g * mixed * factor
    gain_local = jnp.sum(common * opened, axis=0)
    grad_head_low = (common * gain_here * sigma * (1.0 + head_gate * (1.0 - sigma))).astype(BF)
    grad_mixed_low = (
        factor * (gain_here * opened * grad_g) - mixed * (factor * factor * factor) * (along / DV)
    ).astype(BF)

    dq, dk, dv, dcols, drows = mixer_backward(
        q_low, k_low, v_low, cols, rows, states, inverse, w, z, u, grad_mixed_low
    )
    qk_grad = group_exchange(jnp.concatenate([dq, dk], axis=1), group)
    grad_sums = dcols[:, 1].reshape(chunks, CHUNK) + drows.reshape(chunks, 8, CHUNK)[:, 0]
    grad_decay = jnp.flip(jnp.cumsum(jnp.flip(grad_sums, 1), axis=1), 1).reshape(length)
    scalars = group_exchange(jnp.stack([dcols[:, 0], grad_decay]), group)
    grad_projected, grad_gates, conv_local, rate_local, bias_local = front_back(
        (qk_grad[:, :DK], qk_grad[:, DK:], dv.astype(F32), scalars[0], scalars[1])
    )
    only = (place == 0).astype(F32)
    own = jnp.concatenate(
        [
            cut(grad_projected, place * keep, keep),
            grad_projected[:, 2 * DK :],
        ],
        axis=1,
    ).astype(BF)
    grad_gates_low = (grad_gates * only).astype(BF)
    outgoing = jnp.concatenate([own, grad_head_low, grad_gates_low], axis=1)
    weights_here = jnp.concatenate([cut(columns, place * keep, keep), columns[:, 2 * DK :]], axis=1)
    grad_normed_part = lax.dot_general(
        outgoing, weights_here, (((1,), (1,)), ((), ())), preferred_element_type=F32
    )
    first_local = jnp.sum(grad_normed_part * (x_all * scale_all), axis=0)
    grad_normed = lax.psum_scatter(
        grad_normed_part.astype(BF), "ctx", scatter_dimension=0, tiled=True
    ).astype(F32)
    x_scale = lax.rsqrt(jnp.mean(inputs * inputs, axis=-1, keepdims=True) + EPS_NORM)
    weighted = first_full * grad_normed
    inner_mean = jnp.mean(inputs * weighted, axis=-1, keepdims=True)
    input_grad = (
        grad_residual + x_scale * weighted - inputs * (x_scale * x_scale * x_scale) * inner_mean
    )[None]

    front_grad = gram(normed_low, outgoing)
    wide = keep + 2 * width
    front_part = fsdp_sum_rows(front_grad[:, :wide]).astype(BF)
    conv_own = jnp.concatenate([cut(conv_local, place * keep, keep), conv_local[:, 2 * DK :]], axis=1)
    head_slot = lax.dynamic_update_slice(jnp.zeros((DV,), F32), gain_local, (place * width,))
    pieces = [
        front_grad[:, wide:].T.reshape(-1),
        conv_own.reshape(-1),
        first_local,
        second_gain_local,
        head_slot,
        rate_local * only,
        bias_local * only,
    ]
    flat = jnp.concatenate(pieces)
    pad = -flat.shape[0] % wide
    tail = fsdp_sum(jnp.pad(flat, (0, pad))).reshape(-1, wide).astype(BF)
    gathered = lax.all_gather(jnp.concatenate([front_part, tail], axis=0), "ctx").astype(F32)
    main = gathered[:, :shard_rows]
    qk_all = (
        main[:, :, :keep].reshape(H, group, shard_rows, keep).transpose(2, 0, 1, 3).reshape(shard_rows, H, 2, DK)
    )
    value_all = main[:, :, keep : keep + width].transpose(1, 0, 2).reshape(shard_rows, H * DV)
    mixer_grad = jnp.concatenate(
        [qk_all[:, :, 0].reshape(shard_rows, H * DK), qk_all[:, :, 1].reshape(shard_rows, H * DK), value_all],
        axis=1,
    )
    head_gate_grad = main[:, :, keep + width :].transpose(1, 0, 2).reshape(shard_rows, H * DV)
    ends = gathered[:, shard_rows:].reshape(size, -1)
    spots = [0]
    for p in pieces:
        spots.append(spots[-1] + p.shape[0])
    take = lambda i: ends[:, spots[i] : spots[i + 1]]
    mine = lambda a: lax.dynamic_slice_in_dim(a, home * (a.shape[-1] // parts), a.shape[-1] // parts, a.ndim - 1)
    decay_all = jnp.sum(take(0).reshape(H, group, 2, features), axis=1)
    decay_grad = mine(decay_all).transpose(2, 1, 0).reshape(shard_rows, 2 * H)
    conv_all = take(1).reshape(size, KCONV, keep + width)
    conv_qk = (
        conv_all[:, :, :keep].reshape(H, group, KCONV, keep).transpose(2, 0, 1, 3).reshape(KCONV, H, 2, DK)
    )
    conv_grad = mine(
        jnp.concatenate(
            [
                conv_qk[:, :, 0].reshape(KCONV, -1),
                conv_qk[:, :, 1].reshape(KCONV, -1),
                conv_all[:, :, keep:].transpose(1, 0, 2).reshape(KCONV, -1),
            ],
            axis=1,
        )
    )
    first_grad = mine(jnp.sum(take(2), axis=0))
    second_grad = mine(jnp.sum(take(3), axis=0))
    head_grad = mine(jnp.sum(take(4), axis=0))
    rate_grad = mine(jnp.sum(take(5).reshape(H, group), axis=1))
    bias_grad = mine(jnp.sum(take(6).reshape(H, group), axis=1))
    return (
        block_output,
        input_grad,
        mixer_grad,
        decay_grad,
        head_gate_grad,
        merge_grad,
        gate_grad,
        up_grad,
        down_grad,
        conv_grad,
        first_grad,
        head_grad,
        second_grad,
        rate_grad,
        bias_grad,
    )


def solution(mesh):
    tokens = P("fsdp", "ctx", None)
    matrix = P("fsdp", None)
    columns = P(None, "fsdp")
    vector = P("fsdp")
    return jax.shard_map(
        per_device,
        mesh=mesh,
        in_specs=(tokens,) + (matrix,) * 8 + (columns,) + (vector,) * 5 + (tokens,),
        out_specs=(tokens, tokens) + (matrix,) * 7 + (columns,) + (vector,) * 5,
        check_vma=False,
    )
```
